32 devices in a mesh: row: 8 (over y, x, core), col: 4 (over z).
Axes of the slice: x: 2, y: 2, z: 4, core: 2. Of those that a mesh axis runs over, the one named last changes fastest.
Arguments:
- covariance: float32 [2, 8192, 8192], P(None, 'row', 'col'), as said below
- forcing: float32 [2, 8192, 8192], P(None, 'row', 'col'), as said below
- coupling: float32 [2, 64, 64], replicated, may hold values from -0.5 to 0.5
- vertical: float32 [2, 128, 128], replicated, may hold values from -0.375 to 0.375
- damping: float32 [64, 128], replicated, may hold values from 0.3 to 3
- advection: float32 [64, 128], replicated, may hold values from -2 to 2
Outputs:
- advanced: float32 [2, 8192, 8192], P(None, 'row', 'col')
The draws below stay inside these ranges and needn't reach their ends.
Inputs may be any that keep to these rules, and one draw needn't show every extreme that they name: The covariance equals its conjugate transpose: the real plane is symmetric, the imaginary plane antisymmetric. The forcing equals its conjugate transpose: the real plane is symmetric, the imaginary plane antisymmetric.
All inputs are finite; a program needn't handle non-finite values.
Results may differ from the reference program's by a relative error of at most 0.000073.
Values sent between devices are 32-bit elements; how exact they have to be, the bound alone decides.
A program may use at most 320 MiB of HBM per device.

```python
import math
import jax
import jax.numpy as jnp
from jax import lax

NLAT = 64
NZ = 128


def hermitian_draw(key):
    key_real, key_imag = jax.random.split(key, 2)
    matrix_order = NLAT * NZ
    first_plane = jax.random.normal(key_real, (matrix_order, matrix_order), jnp.float32)
    second_plane = jax.random.normal(key_imag, (matrix_order, matrix_order), jnp.float32)
    real_part = (first_plane + first_plane.T) * 0.5
    imag_part = (second_plane - second_plane.T) * 0.5
    return jnp.stack([real_part, imag_part])


def draw_covariance(key, part):
    return hermitian_draw(jax.random.fold_in(key, 11))


def draw_forcing(key, part):
    return hermitian_draw(jax.random.fold_in(key, 23))


def gaussian(rng, extent, width, limit, held_as=jnp.bfloat16):
    drawn = width * jax.random.normal(rng, extent, jnp.float32)
    return jnp.clip(drawn, min=-limit, max=limit).astype(held_as)


def setup_inputs(seed: int = 0) -> dict:
    seeds = jax.random.split(jax.random.key(seed), 7)
    covariance = draw_covariance(jax.random.fold_in(seeds[6], 71), 0)
    forcing = draw_forcing(jax.random.fold_in(seeds[6], 71), 0)
    coupling = gaussian(seeds[2], (2, NLAT, NLAT), (2 * NLAT) ** -0.5, 0.5, jnp.float32)
    vertical = gaussian(seeds[3], (2, NZ, NZ), (2 * NZ) ** -0.5, 0.375, jnp.float32)
    damping = jnp.clip(jnp.exp(jax.random.uniform(seeds[4], (NLAT, NZ), jnp.float32, math.log(0.3), math.log(3.0))), 0.3, 3.0)
    advection = jnp.clip(jax.random.uniform(seeds[5], (NLAT, NZ), jnp.float32, -2.0, 2.0), -2.0, 2.0)
    return {"covariance": covariance, "forcing": forcing, "coupling": coupling, "vertical": vertical, "damping": damping, "advection": advection}


step_size = 0.25


def complex_einsum(pattern, factor, values):
    def single(factor_part, value_part):
        return jnp.einsum(pattern, factor_part, value_part, precision=lax.Precision.HIGHEST)
    real_part = single(factor[0], values[0]) - single(factor[1], values[1])
    imag_part = single(factor[0], values[1]) + single(factor[1], values[0])
    return jnp.stack([real_part, imag_part])


def complex_scale(factor, values):
    real_part = factor[0] * values[0] - factor[1] * values[1]
    imag_part = factor[0] * values[1] + factor[1] * values[0]
    return jnp.stack([real_part, imag_part])


def conjugate(values):
    return jnp.stack([values[0], -values[1]])


def left_apply(by_rows, coupling, vertical, rates):
    total = complex_einsum('lm,amj->alj', vertical, by_rows)
    total = total + complex_einsum('ab,blj->alj', coupling, by_rows)
    return total + complex_scale(rates[:, :, :, None], by_rows)


def right_apply(by_cols, coupling, vertical, rates):
    total = complex_einsum('lm,iam->ial', conjugate(vertical), by_cols)
    total = total + complex_einsum('ab,ibl->ial', conjugate(coupling), by_cols)
    return total + complex_scale(conjugate(rates)[:, None], by_cols)


def tendency(matrix, forcing, coupling, vertical, rates):
    matrix_order = matrix.shape[1]
    lat_count = coupling.shape[1]
    levels = vertical.shape[1]
    left_term = left_apply(matrix.reshape(2, lat_count, levels, matrix_order), coupling, vertical, rates)
    right_term = right_apply(matrix.reshape(2, matrix_order, lat_count, levels), coupling, vertical, rates)
    return left_term.reshape(2, matrix_order, matrix_order) + right_term.reshape(2, matrix_order, matrix_order) + forcing


def reference(covariance, forcing, coupling, vertical, damping, advection):
    rates = jnp.stack([-damping, advection])
    first_rate = tendency(covariance, forcing, coupling, vertical, rates)
    midpoint = covariance + (0.5 * step_size) * first_rate
    return covariance + step_size * tendency(midpoint, forcing, coupling, vertical, rates)
```

```python
import jax
import jax.numpy as jnp
from jax import lax
from jax.sharding import PartitionSpec as P

step_size = 0.25


def real_form(matrix):
    re, im = matrix
    top = jnp.stack([re, -im], axis=-2)
    bottom = jnp.stack([im, re], axis=-2)
    return jnp.stack([top, bottom], axis=-4)


def shards(row_size, col_size, covariance, forcing, coupling, vertical, damping, advection):
    rows_here, cols_here = covariance.shape[1:]
    lats, levels = damping.shape
    lats_row = rows_here // levels
    groups = cols_here // rows_here
    width = rows_here // row_size
    cols = groups * width

    eye = jnp.eye(levels, dtype=jnp.float32)
    level_op = real_form(
        (
            vertical[0] - damping[:, :, None] * eye,
            vertical[1] + advection[:, :, None] * eye,
        )
    ).reshape(lats, 2 * levels, 2 * levels)
    lat_op = jnp.moveaxis(real_form(coupling), (0, 1, 2, 3), (1, 0, 3, 2)).reshape(2 * lats, 2 * lats)

    def to_columns(tile):
        split = tile.reshape(2, lats_row, levels, groups, row_size, width)
        split = split.transpose(4, 1, 0, 2, 3, 5).reshape(row_size * lats_row, 2, levels, cols)
        return lax.all_to_all(split, "row", split_axis=0, concat_axis=0, tiled=True)

    def to_tile(block):
        parts = lax.all_to_all(block, "row", split_axis=0, concat_axis=0, tiled=True)
        parts = parts.reshape(row_size, lats_row, 2, levels, groups, width)
        return parts.transpose(2, 1, 3, 4, 0, 5).reshape(2, rows_here, cols_here)

    def left(block):
        by_level = jnp.einsum(
            "axy,ayj->axj",
            level_op,
            block.reshape(lats, 2 * levels, cols),
            precision=lax.Precision.HIGH,
        ).reshape(block.shape)
        by_lat = jnp.einsum(
            "xy,ylj->xlj",
            lat_op,
            block.reshape(2 * lats, levels, cols),
            precision=lax.Precision.HIGH,
        ).reshape(block.shape)
        return by_level + by_lat

    def adjoint(block):
        planes = block.transpose(1, 0, 2, 3).reshape(2, col_size, groups, row_size, width, cols)
        send = planes.transpose(1, 3, 0, 5, 2, 4).reshape(col_size * row_size, 2, cols, cols)
        got = lax.all_to_all(send, ("col", "row"), split_axis=0, concat_axis=0, tiled=True)
        got = got.reshape(col_size, row_size, 2, groups, width, cols)
        got = got.transpose(2, 0, 3, 1, 4, 5).reshape(2, lats, levels, cols)
        return jnp.stack([got[0], -got[1]], axis=1)

    cov = to_columns(covariance)
    force = to_columns(forcing)
    first = left(cov)
    midpoint = cov + (0.5 * step_size) * (first + adjoint(first) + force)
    second = left(midpoint)
    return to_tile(cov + step_size * (second + adjoint(second) + force))


def solution(mesh):
    row_size, col_size = mesh.shape["row"], mesh.shape["col"]

    def body(*args):
        return shards(row_size, col_size, *args)

    return jax.shard_map(
        body,
        mesh=mesh,
        in_specs=(P(None, "row", "col"), P(None, "row", "col"), P(), P(), P(), P()),
        out_specs=P(None, "row", "col"),
        check_vma=False,
    )
```
